32 devices in a mesh: ctx: 4 (over z), head: 4 (over x, core), rep: 2 (over y).
Axes of the slice: x: 2, y: 2, z: 4, core: 2. Of those that a mesh axis runs over, the one named last changes fastest.
Arguments:
- queries: bfloat16 [4, 256, 2048], P('rep', 'ctx', 'head'), may hold values from -6 to 6
- keyvals: bfloat16 [4, 256, 4, 128], P('rep', 'ctx', 'head'), may hold values from -6 to 6
- sinks: float32 [32], P('head'), may hold values from -1 to 3
- stream: bfloat16 [4, 256, 2880], P('rep', 'ctx', 'head'), may hold values from -6 to 6
- out_weight: bfloat16 [2048, 2880], P('head', 'ctx'), may hold values from -0.75 to 0.75
- norm_gain: float32 [2880], replicated, may hold values from 0.1 to 1.9
- router: bfloat16 [2880, 32], replicated, may hold values from -0.12 to 0.12
- expert_ids: int32 [4, 256, 4], P('rep', 'ctx'), may hold values from 0 to 31, all different within a row; in each aligned block of 64 rows (0 to 63, 64 to 127, ..., all dimensions but the last counted through in order) at most 12 rows name the same one
- w_gate_up: bfloat16 [64, 720, 5760], P('ctx', 'head'), may hold values from -0.109375 to 0.109375
- w_down: bfloat16 [64, 720, 2880], P('ctx', None, 'head'), may hold values from -0.15625 to 0.15625
Outputs:
- layer_out: bfloat16 [4, 256, 2880], P('rep', 'ctx', 'head')
The draws below stay inside these ranges and needn't reach their ends.
Inputs may be any that keep to these rules, and one draw needn't show every extreme that they name: `expert_ids`: each position names 4 different experts. Within each aligned block of 64 positions of a sequence no expert is named by more than 12 positions, and in every draw some block has an expert named by exactly 12.
All inputs are finite; a program needn't handle non-finite values.
Results may differ from the reference program's by a relative error of at most 0.015.
Values may be sent and summed in bfloat16 or wider, within the bound.
A program may use at most 192 MiB of HBM per device.

```python
import math
import jax
import jax.numpy as jnp
import numpy as np
from jax import lax

D = 2880
HEAD_SIZE = 64
QUERY_HEADS = 32
KEYVALUE_HEADS = 4
H = 1440
EXPERTS = 32
TOPK = 4
SEQUENCE_COUNT = 4
SEQUENCE_LENGTH = 256
BLOCK = 64
CAP = 12


def drawn_draw(key):
    base_key = jax.random.fold_in(key, 29)
    key_query, key_keys, key_values = jax.random.split(base_key, 3)
    shape_query = (SEQUENCE_COUNT, SEQUENCE_LENGTH, QUERY_HEADS, HEAD_SIZE)
    key_tensor_shape = (SEQUENCE_COUNT, SEQUENCE_LENGTH, KEYVALUE_HEADS, HEAD_SIZE)
    query_vals = jnp.clip(jax.random.normal(key_query, shape_query, jnp.float32), -5.0, 5.0)
    key_vals = jnp.clip(jax.random.normal(key_keys, key_tensor_shape, jnp.float32), -5.0, 5.0)
    value_vals = jnp.clip(jax.random.normal(key_values, key_tensor_shape, jnp.float32), -5.0, 5.0)
    return (query_vals, key_vals, value_vals)


def draw_queries(key, part):
    query_vals, key_vals, value_vals = drawn_draw(key)
    return query_vals.reshape(SEQUENCE_COUNT, SEQUENCE_LENGTH, QUERY_HEADS * HEAD_SIZE).astype(jnp.bfloat16)


def draw_keyvals(key, part):
    query_vals, key_vals, value_vals = drawn_draw(key)
    return jnp.concatenate([key_vals, value_vals], axis=-1).astype(jnp.bfloat16)


def draw_router(key, part):
    key_noise = jax.random.fold_in(jax.random.fold_in(key, 43), 0)
    values = jnp.clip(jax.random.normal(key_noise, (D, EXPERTS), jnp.float32), -5.0, 5.0) * D ** (-0.5)
    return values.astype(jnp.bfloat16)


def draw_stream(key, part):
    key_noise = jax.random.fold_in(jax.random.fold_in(key, 47), 0)
    shape_stream = (SEQUENCE_COUNT, SEQUENCE_LENGTH, D)
    values = jnp.clip(jax.random.normal(key_noise, shape_stream, jnp.float32), -6.0, 6.0)
    return values.astype(jnp.bfloat16)


def shard_levels(rng, dims, cuts, smallest, high):
    factor_of, own = 1.0, jax.random.fold_in(rng, 6)
    for axis_at, shards_of in cuts:
        steps = jnp.exp(jax.random.uniform(jax.random.fold_in(own, axis_at), (shards_of,), jnp.float32, smallest / len(cuts), high / len(cuts)))
        factor_of = factor_of * jnp.repeat(steps, dims[axis_at] // shards_of).reshape([-1 if axis == axis_at else 1 for axis in range(len(dims))])
    return factor_of


def routed_block(stream_key, own, number, rows, number_of, top, most, slope):
    ranking = jax.random.permutation(stream_key, number_of)
    heavy_load, usual = portions_of(number_of, rows * top, most, slope, True), portions_of(number_of, rows * top, most, slope, False)
    places = jnp.arange(number_of)

    def named(sizes, offset_by):
        used = int((sizes > 0).sum())
        fixed = max(1, used // 4)
        moved = fixed + (places - fixed + offset_by * (used - fixed)) % max(1, number_of - fixed)
        return jnp.zeros((number_of,), jnp.int32).at[ranking[jnp.where(places < fixed, places, moved)]].set(jnp.asarray(sizes, jnp.int32))

    sizes = jnp.where(number % 4 == 0, named(heavy_load, number // 4), named(usual, number - number // 4 - 1))
    mixed = jax.random.permutation(jax.random.fold_in(own, 3), number_of)
    source_of, sink = mixed[0:number_of // 2 * 2:2], mixed[1:number_of // 2 * 2:2]
    room = jnp.minimum(sizes[source_of] - 1, most - sizes[sink]) // 2
    room = jnp.where((source_of == ranking[0]) | (sink == ranking[0]) | (sizes[sink] == 0), 0, jnp.maximum(room, 0))
    moved = jax.random.randint(jax.random.fold_in(own, 4), (number_of // 2,), 0, 1 << 20) % (room + 1)
    sizes = sizes.at[source_of].add(-moved).at[sink].add(moved)
    members = jnp.searchsorted(jnp.cumsum(sizes), jnp.arange(rows * top), side="right").astype(jnp.int32)
    listing = members.reshape(top, rows).T
    listing = listing[jax.random.permutation(jax.random.fold_in(own, 1), rows)]
    offset_by = jax.random.randint(jax.random.fold_in(own, 2), (rows, 1), 0, top)
    return jnp.take_along_axis(listing, (jnp.arange(top)[None, :] + offset_by) % top, axis=1)


def portions_of(count, total, most, skew, full):
    loads = [(1 << 20) // math.isqrt(grade ** skew) + 1 for grade in range(1, count + 1)]
    largest = most if full else min(most, max(-(-total // count), total * loads[0] // sum(loads)))
    least = 1 if total - largest >= count - 1 else 0
    holding, spare = [largest] + [least] * (count - 1), total - largest - least * (count - 1)
    while spare > 0:
        free = [i for i in range(1, count) if holding[i] < largest] or [i for i in range(1, count) if holding[i] < most]
        pool, budget = sum([loads[i] for i in free]), spare
        for i in free:
            addition = min(most - holding[i], max(1, budget * loads[i] // pool), spare)
            holding[i] = holding[i] + addition
            spare = spare - addition
    return np.array(holding)


def scatter_about(rng, dims, spread, most, cuts=(), kind=jnp.bfloat16):
    level = shard_levels(rng, dims, cuts, -0.22, 0.18) if cuts else 1.0
    drawn = jax.random.normal(rng, dims, jnp.float32) * spread * level
    return jnp.minimum(jnp.maximum(drawn, -most), most).astype(kind)


def setup_inputs(seed: int = 0) -> dict:
    key_of = jax.random.split(jax.random.key(seed), 11)
    queries = draw_queries(jax.random.fold_in(key_of[10], 71), 0)
    keyvals = draw_keyvals(jax.random.fold_in(key_of[10], 71), 0)
    sinks = jnp.clip(-1.0 + 4.0 * jax.random.uniform(key_of[2], (QUERY_HEADS,), jnp.float32) ** shard_levels(key_of[2], (QUERY_HEADS,), ((0, 4),), -0.2, 0.2), -1.0, 3.0)
    stream = draw_stream(jax.random.fold_in(key_of[10], 71), 0)
    out_weight = scatter_about(key_of[4], (QUERY_HEADS * HEAD_SIZE, D), HEAD_SIZE ** -0.5, 0.75, ((0, 4), (1, 4)))
    norm_gain = jnp.clip(1.0 + 0.18 * jax.random.normal(key_of[5], (D,), jnp.float32), 0.1, 1.9)
    router = draw_router(jax.random.fold_in(key_of[10], 71), 0)
    expert_ids_keys = jax.random.split(jax.random.fold_in(key_of[7], 1), SEQUENCE_COUNT * SEQUENCE_LENGTH // BLOCK)
    expert_ids_turns = jax.random.permutation(jax.random.fold_in(key_of[7], 3), SEQUENCE_COUNT * SEQUENCE_LENGTH // BLOCK)
    expert_ids = jax.vmap(lambda own, number: routed_block(jax.random.fold_in(key_of[7], 2), own, number, BLOCK, EXPERTS, TOPK, CAP, 2))(expert_ids_keys, expert_ids_turns).reshape((SEQUENCE_COUNT, SEQUENCE_LENGTH, TOPK))
    w_gate_up = scatter_about(key_of[8], (2 * EXPERTS, H // 2, 2 * D), D ** -0.5, 0.109375, ((0, 4), (1, 4)))
    w_down = scatter_about(key_of[9], (2 * EXPERTS, H // 2, D), H ** -0.5, 0.15625, ((0, 4), (2, 4)))
    return {"queries": queries, "keyvals": keyvals, "sinks": sinks, "stream": stream, "out_weight": out_weight, "norm_gain": norm_gain, "router": router, "expert_ids": expert_ids, "w_gate_up": w_gate_up, "w_down": w_down}


def attend_sequence(query_seq, keyval_seq, sinks):
    length = query_seq.shape[0]
    query_heads = query_seq.reshape(length, QUERY_HEADS, HEAD_SIZE)
    key_heads = keyval_seq[:, :, :HEAD_SIZE]
    value_heads = keyval_seq[:, :, HEAD_SIZE:]
    query_group_size = QUERY_HEADS // KEYVALUE_HEADS
    causal = jnp.arange(length)[None, :] <= jnp.arange(length)[:, None]

    def one_head(head_index):
        query_mat = lax.dynamic_index_in_dim(query_heads, head_index, 1, keepdims=False)
        kv_index = head_index // query_group_size
        key_mat = lax.dynamic_index_in_dim(key_heads, kv_index, 1, keepdims=False)
        value_mat = lax.dynamic_index_in_dim(value_heads, kv_index, 1, keepdims=False)
        scores = jnp.dot(query_mat, key_mat.T, preferred_element_type=jnp.float32) * HEAD_SIZE ** (-0.5)
        sink_value = lax.dynamic_index_in_dim(sinks, head_index, 0, keepdims=False)
        peak = jnp.maximum(sink_value, lax.optimization_barrier(jnp.max(jnp.where(causal, scores, -jnp.inf), axis=-1)))
        exp_terms = jnp.where(causal, jnp.exp(scores - peak[:, None]), 0.0)
        total = jnp.exp(sink_value - peak) + lax.optimization_barrier(jnp.sum(exp_terms, axis=-1))
        weighted = jnp.dot(exp_terms.astype(jnp.bfloat16), value_mat, preferred_element_type=jnp.float32)
        return (weighted / total[:, None]).astype(jnp.bfloat16)
    heads_out = lax.map(one_head, jnp.arange(QUERY_HEADS, dtype=jnp.int32))
    return jnp.transpose(heads_out, (1, 0, 2)).reshape(length, QUERY_HEADS * HEAD_SIZE)

def reference(queries, keyvals, sinks, stream, out_weight, norm_gain, router, expert_ids, w_gate_up, w_down):
    attended = jnp.stack([attend_sequence(queries[seq_index], keyvals[seq_index], sinks) for seq_index in range(SEQUENCE_COUNT)])
    flat_attended = attended.reshape(SEQUENCE_COUNT * SEQUENCE_LENGTH, QUERY_HEADS * HEAD_SIZE)
    projected = jnp.dot(flat_attended, out_weight, preferred_element_type=jnp.float32)
    hidden_state = (stream.reshape(SEQUENCE_COUNT * SEQUENCE_LENGTH, D).astype(jnp.float32) + projected).astype(jnp.bfloat16)
    state_float = hidden_state.astype(jnp.float32)
    inverse = lax.rsqrt(lax.optimization_barrier(jnp.mean(state_float * state_float, axis=-1, keepdims=True)) + 1e-05)
    normed = (state_float * inverse * norm_gain).astype(jnp.bfloat16)
    logits = jnp.dot(normed, router, preferred_element_type=jnp.float32)
    chosen_ids = expert_ids.reshape(SEQUENCE_COUNT * SEQUENCE_LENGTH, TOPK)
    chosen = jnp.take_along_axis(logits, chosen_ids, axis=1)
    mix_weights = jax.nn.softmax(chosen, axis=-1)
    bound = SEQUENCE_COUNT * SEQUENCE_LENGTH // BLOCK * CAP
    pair_experts = chosen_ids.reshape(-1)
    pair_mix = mix_weights.reshape(-1)

    def one_row(running, weight_row):
        expert = weight_row // 2
        is_member = pair_experts == expert
        picked = jnp.nonzero(is_member, size=bound, fill_value=0)[0].astype(jnp.int32)
        member_count = jnp.sum(is_member.astype(jnp.int32))
        valid = jnp.arange(bound, dtype=jnp.int32) < member_count
        token_rows = picked // TOPK
        inputs = normed[token_rows]
        weights_in = lax.dynamic_index_in_dim(w_gate_up, weight_row, 0, keepdims=False).reshape(H // 2, 2, D)
        gate_part = jnp.dot(inputs, weights_in[:, 0, :].T, preferred_element_type=jnp.float32)
        up_part = jnp.dot(inputs, weights_in[:, 1, :].T, preferred_element_type=jnp.float32)
        active = (gate_part * jax.nn.sigmoid(1.702 * gate_part) * (up_part + 1.0)).astype(jnp.bfloat16)
        weights_out = lax.dynamic_index_in_dim(w_down, weight_row, 0, keepdims=False)
        part_out = jnp.dot(active, weights_out, preferred_element_type=jnp.float32).astype(jnp.bfloat16)
        scale = jnp.where(valid, pair_mix[picked], 0.0)
        running = running.at[token_rows].add(scale[:, None] * part_out.astype(jnp.float32))
        return (running, None)
    experts_out, unused = lax.scan(one_row, jnp.zeros((SEQUENCE_COUNT * SEQUENCE_LENGTH, D), jnp.float32), jnp.arange(2 * EXPERTS, dtype=jnp.int32))
    layer_out = (state_float + experts_out).astype(jnp.bfloat16)
    return layer_out.reshape(SEQUENCE_COUNT, SEQUENCE_LENGTH, D)
```

```python
import functools

import jax
import jax.numpy as jnp
from jax import lax
from jax.experimental import pallas as pl
from jax.experimental.pallas import tpu as pltpu
from jax.sharding import PartitionSpec as P


NT = (((1,), (1,)), ((), ()))
TN = (((0,), (0,)), ((), ()))
LANES = 128


def one_hot_rows(slots, cap, value):
    rows = lax.broadcasted_iota(jnp.int32, (cap, slots.shape[1]), 0)
    return jnp.where(rows == slots, value, 0.0).astype(jnp.bfloat16)


def gate_up_kernel(
    halves,
    units,
    state_ref,
    gain_ref,
    router_ref,
    w_ref,
    slot_ref,
    out_ref,
    logits_ref,
    act_ref,
    xg_ref,
    xu_ref,
):
    step = pl.program_id(1)
    groups, shards, group_rows, cols = state_ref.shape

    @pl.when(step == 0)
    def _():
        for group in range(groups):
            pieces = [state_ref[group, shard].astype(jnp.float32) for shard in range(shards)]
            square = sum(jnp.sum(piece * piece, axis=1, keepdims=True) for piece in pieces)
            inverse = lax.rsqrt(square / (shards * cols) + 1e-05)
            scaled = [
                (piece * inverse * gain_ref[shard]).astype(jnp.bfloat16)
                for shard, piece in enumerate(pieces)
            ]
            extra = xg_ref.shape[1] - shards * cols
            blank = [jnp.zeros((group_rows, extra), jnp.bfloat16)] if extra else []
            here = slice(group * group_rows, (group + 1) * group_rows)
            xg_ref[here, :] = jnp.concatenate(scaled + blank, axis=1)
            xu_ref[here, :] = jnp.concatenate(blank + scaled, axis=1)
        logits_ref[...] = lax.dot_general(
            router_ref[...], xg_ref[...], NT, preferred_element_type=jnp.float32
        )

    rows, wide = w_ref.shape[0], xg_ref.shape[1]
    gate = lax.dot_general(w_ref[:, :wide], xg_ref[...], NT, preferred_element_type=jnp.float32)
    up = lax.dot_general(
        w_ref[:, w_ref.shape[1] - wide :], xu_ref[...], NT, preferred_element_type=jnp.float32
    )
    active = gate * jax.nn.sigmoid(1.702 * gate) * (up + 1.0)
    slabs = act_ref.shape[0]
    for slab in range(slabs):
        act_ref[slab, pl.ds(step * rows, rows), :] = active[:, slab * LANES : (slab + 1) * LANES]

    @pl.when(step == pl.num_programs(1) - 1)
    def _():
        for row in range(halves):
            wanted = pl.ds(row, units, stride=halves) if halves > 1 else pl.ds(0, units)
            picked = jnp.concatenate([act_ref[slab, wanted, :] for slab in range(slabs)], axis=1)
            spread = one_hot_rows(slot_ref[row], out_ref.shape[2], 1.0)
            out_ref[row, 0] = lax.dot_general(
                spread, picked.astype(jnp.bfloat16), NT, preferred_element_type=jnp.float32
            ).astype(jnp.bfloat16)


def gate_up_call(state, gain, router, weights, slots, units, token_block, cap):
    halves = slots.shape[0]
    sources, shards, group_rows, cols = state.shape
    groups = token_block // group_rows
    blocks = sources // groups
    experts, wide = router.shape
    wide_w = weights.shape[1]
    sizes = [
        size
        for size in range(1, units + 1)
        if units % size == 0
        and (size == units or (size * halves) % 16 == 0)
        and size * halves * wide_w * 2 <= 4 << 20
    ]
    size = sizes[-1]
    return pl.pallas_call(
        functools.partial(gate_up_kernel, halves, units),
        grid=(blocks, units // size),
        out_shape=(
            jax.ShapeDtypeStruct((halves, blocks, cap, units), jnp.bfloat16),
            jax.ShapeDtypeStruct((experts, blocks * token_block), jnp.float32),
        ),
        in_specs=[
            pl.BlockSpec((groups, shards, group_rows, cols), lambda i, j: (i, 0, 0, 0)),
            pl.BlockSpec((shards, 1, cols), lambda i, j: (0, 0, 0)),
            pl.BlockSpec((experts, wide), lambda i, j: (0, 0)),
            pl.BlockSpec((size * halves, wide_w), lambda i, j: (j, 0)),
            pl.BlockSpec((halves, 1, token_block), lambda i, j: (0, 0, i)),
        ],
        out_specs=(
            pl.BlockSpec((halves, 1, cap, units), lambda i, j: (0, i, 0, 0)),
            pl.BlockSpec((experts, token_block), lambda i, j: (0, i)),
        ),
        scratch_shapes=[
            pltpu.VMEM((token_block // LANES, units * halves, LANES), jnp.float32),
            pltpu.VMEM((token_block, wide), jnp.bfloat16),
            pltpu.VMEM((token_block, wide), jnp.bfloat16),
        ],
        compiler_params=pltpu.CompilerParams(vmem_limit_bytes=56 << 20),
    )(state, gain, router, weights, slots)


def down_kernel(act_ref, place_ref, w_ref, slot_ref, mix_ref, out_ref, total_ref):
    row = pl.program_id(1)
    hidden = None
    for shard in range(act_ref.shape[0]):
        piece = jnp.dot(
            act_ref[shard, 0, 0], place_ref[shard], preferred_element_type=jnp.float32
        )
        hidden = piece if hidden is None else hidden + piece
    part = jnp.dot(hidden.astype(jnp.bfloat16), w_ref[0], preferred_element_type=jnp.float32)
    spread = one_hot_rows(slot_ref[0], act_ref.shape[3], mix_ref[0])
    added = lax.dot_general(
        spread, part.astype(jnp.bfloat16), TN, preferred_element_type=jnp.float32
    )

    @pl.when(row == 0)
    def _():
        total_ref[...] = added

    @pl.when(row != 0)
    def _():
        total_ref[...] += added

    @pl.when(row == pl.num_programs(1) - 1)
    def _():
        out_ref[...] = total_ref[...].astype(jnp.bfloat16)


def down_call(act, weights, slots, mix, token_block):
    shards, halves, blocks, cap, units = act.shape
    hidden, cols = weights.shape[1:]
    at = lax.broadcasted_iota(jnp.int32, (shards, units, hidden), 0) * units
    at = at + lax.broadcasted_iota(jnp.int32, (shards, units, hidden), 1)
    place = (at == lax.broadcasted_iota(jnp.int32, (shards, units, hidden), 2)).astype(jnp.bfloat16)
    return pl.pallas_call(
        down_kernel,
        grid=(blocks, halves),
        out_shape=jax.ShapeDtypeStruct((blocks * token_block, cols), jnp.bfloat16),
        in_specs=[
            pl.BlockSpec((shards, 1, 1, cap, units), lambda i, r: (0, r, i, 0, 0)),
            pl.BlockSpec((shards, units, hidden), lambda i, r: (0, 0, 0)),
            pl.BlockSpec((1, hidden, cols), lambda i, r: (r, 0, 0)),
            pl.BlockSpec((1, 1, token_block), lambda i, r: (r, 0, i)),
            pl.BlockSpec((1, 1, token_block), lambda i, r: (r, 0, i)),
        ],
        out_specs=pl.BlockSpec((token_block, cols), lambda i, r: (i, 0)),
        scratch_shapes=[pltpu.VMEM((token_block, cols), jnp.float32)],
        compiler_params=pltpu.CompilerParams(vmem_limit_bytes=48 << 20),
    )(act, place, weights, slots, mix)


def on_device(
    queries, keyvals, sinks, stream, out_weight, norm_gain, router, expert_ids, w_gate_up, w_down
):
    ctx_count = lax.axis_size("ctx")
    local_seqs = queries.shape[0]
    tokens = queries.shape[1]
    row_count = local_seqs * tokens
    kv_local = keyvals.shape[2]
    head_dim = keyvals.shape[3] // 2
    q_local = queries.shape[2] // head_dim
    query_group_size = q_local // kv_local
    wide_rows = query_group_size * tokens
    col_width = stream.shape[2]
    first_pos = lax.axis_index("ctx") * tokens
    last_pos = first_pos + tokens - 1
    score_scale = head_dim ** (-0.5)
    scaled_queries = queries * jnp.asarray(score_scale, jnp.bfloat16)
    query_grid = scaled_queries.reshape(local_seqs, tokens, kv_local, query_group_size, head_dim)
    query_wide = jnp.transpose(query_grid, (0, 2, 3, 1, 4)).reshape(
        local_seqs, kv_local, wide_rows, head_dim
    )
    positions = first_pos + jnp.tile(jnp.arange(tokens), query_group_size)
    sink_rows = jnp.repeat(sinks.reshape(kv_local, query_group_size), tokens, axis=1)
    sink_grid = jnp.broadcast_to(sink_rows[None], (local_seqs, kv_local, wide_rows))
    start_state = (
        sink_grid,
        jnp.ones_like(sink_grid),
        jnp.zeros((local_seqs, kv_local, head_dim, wide_rows), jnp.float32),
    )

    def attend_block(running, shard_piece):
        peak_old, denom_old, accum_old = running
        key_block = shard_piece[..., :head_dim]
        value_block = shard_piece[..., head_dim:]
        scores = jnp.einsum(
            "skmd,snkd->sknm", query_wide, key_block, preferred_element_type=jnp.float32
        )
        key_pos = jnp.arange(shard_piece.shape[1])
        visible = key_pos[:, None] <= positions[None, :]
        masked = jnp.where(visible[None, None], scores, -jnp.inf)
        peak_new = jnp.maximum(peak_old, jnp.max(masked, axis=2))
        exp_terms = jnp.exp(masked - peak_new[:, :, None, :])
        factor = jnp.exp(peak_old - peak_new)
        denom_new = denom_old * factor + jnp.sum(exp_terms, axis=2)
        accum_new = accum_old * factor[:, :, None, :] + jnp.einsum(
            "sknm,snkd->skdm",
            exp_terms.astype(jnp.bfloat16),
            value_block,
            preferred_element_type=jnp.float32,
        )
        return (peak_new, denom_new, accum_new)

    shard_piece = lax.all_gather(keyvals, "ctx", axis=1, tiled=True)

    def keep_state(state_in):
        return state_in

    def update_state(state_in):
        return attend_block(state_in, shard_piece)

    peak_fin, denom_fin, accum_fin = lax.cond(
        jnp.int32(0) > last_pos, keep_state, update_state, start_state
    )
    normalized = (accum_fin / denom_fin[:, :, None, :]).reshape(
        local_seqs, kv_local, head_dim, query_group_size, tokens
    )
    attended = (
        jnp.transpose(normalized, (0, 4, 1, 3, 2))
        .reshape(row_count, q_local * head_dim)
        .astype(jnp.bfloat16)
    )
    partial_proj = jnp.dot(
        attended,
        lax.all_gather(out_weight, "ctx", axis=1, tiled=True),
        preferred_element_type=jnp.float32,
    )
    own_stream = stream.reshape(row_count, col_width).astype(jnp.float32)
    summed = lax.psum_scatter(
        partial_proj.astype(jnp.bfloat16), "head", scatter_dimension=1, tiled=True
    )
    own_state = (summed.astype(jnp.float32) + own_stream).astype(jnp.bfloat16)
    width = norm_gain.shape[0]
    every_state = lax.all_gather(own_state, ("ctx", "head"), axis=0, tiled=False)
    every_state = every_state.reshape(ctx_count, width // col_width, row_count, col_width)
    all_rows = ctx_count * row_count
    expert_count = router.shape[1]
    token_ids = lax.all_gather(
        expert_ids.reshape(row_count, expert_ids.shape[2]).T, "ctx", axis=1, tiled=True
    )
    halves = w_gate_up.shape[0]
    units = w_gate_up.shape[1]
    token_block = min(all_rows, 8 * tokens)
    cap = token_block // tokens * (3 * tokens // 16)
    row_expert = (lax.axis_index("ctx") * halves + jnp.arange(halves)) // 2
    named = jnp.any(token_ids[:, None, :] == row_expert[None, :, None], axis=0)
    counted = named.astype(jnp.int32).reshape(halves, all_rows // token_block, token_block)
    rank = jnp.cumsum(counted, axis=2) - 1
    slots = jnp.where(named, rank.reshape(halves, all_rows), -1).reshape(halves, 1, all_rows)
    unit_rows = jnp.transpose(w_gate_up, (1, 0, 2)).reshape(units * halves, w_gate_up.shape[2])
    router_rows = jnp.pad(router.T, ((0, 0), (0, -width % LANES)))
    gain = norm_gain.reshape(width // col_width, 1, col_width)
    active, logits = gate_up_call(
        every_state, gain, router_rows, unit_rows, slots, units, token_block, cap
    )
    member = jnp.any(token_ids[:, None, :] == jnp.arange(expert_count)[None, :, None], axis=0)
    masked = jnp.where(member, logits, -jnp.inf)
    mix_all = jax.nn.softmax(masked, axis=0)
    chosen_rows = (row_expert[:, None] == jnp.arange(expert_count)[None, :]).astype(jnp.float32)
    mix_rows = jnp.dot(chosen_rows, mix_all, precision=lax.Precision.HIGHEST)
    mix_rows = mix_rows.reshape(halves, 1, all_rows)
    every_active = lax.all_gather(active, "head", axis=0, tiled=False)
    partial_out = down_call(every_active, w_down, slots, mix_rows, token_block)
    combined = lax.psum_scatter(partial_out, "ctx", scatter_dimension=0, tiled=True)
    layer_out = (own_state.astype(jnp.float32) + combined.astype(jnp.float32)).astype(jnp.bfloat16)
    return layer_out.reshape(local_seqs, tokens, col_width)


def solution(mesh):
    placed = (
        P("rep", "ctx", "head"),
        P("rep", "ctx", "head", None),
        P("head"),
        P("rep", "ctx", "head"),
        P("head", "ctx"),
        P(),
        P(),
        P("rep", "ctx", None),
        P("ctx", "head", None),
        P("ctx", None, "head"),
    )
    return jax.shard_map(
        on_device, mesh=mesh, in_specs=placed, out_specs=P("rep", "ctx", "head"), check_vma=False
    )
```

```python
import functools

import jax
import jax.numpy as jnp
from jax import lax
from jax.experimental import pallas as pl
from jax.experimental.pallas import tpu as pltpu
from jax.sharding import PartitionSpec as P


NT = (((1,), (1,)), ((), ()))
TN = (((0,), (0,)), ((), ()))
LANES = 128


def one_hot_rows(slots, cap, value):
    rows = lax.broadcasted_iota(jnp.int32, (cap, slots.shape[1]), 0)
    return jnp.where(rows == slots, value, 0.0).astype(jnp.bfloat16)


def gate_up_kernel(
    halves,
    units,
    state_ref,
    gain_ref,
    router_ref,
    w_ref,
    slot_ref,
    out_ref,
    logits_ref,
    act_ref,
    xg_ref,
    xu_ref,
):
    step = pl.program_id(1)
    groups, shards, group_rows, cols = state_ref.shape

    @pl.when(step == 0)
    def _():
        for group in range(groups):
            pieces = [state_ref[group, shard].astype(jnp.float32) for shard in range(shards)]
            square = sum(jnp.sum(piece * piece, axis=1, keepdims=True) for piece in pieces)
            inverse = lax.rsqrt(square / (shards * cols) + 1e-05)
            scaled = [
                (piece * inverse * gain_ref[shard]).astype(jnp.bfloat16)
                for shard, piece in enumerate(pieces)
            ]
            extra = xg_ref.shape[1] - shards * cols
            blank = [jnp.zeros((group_rows, extra), jnp.bfloat16)] if extra else []
            here = slice(group * group_rows, (group + 1) * group_rows)
            xg_ref[here, :] = jnp.concatenate(scaled + blank, axis=1)
            xu_ref[here, :] = jnp.concatenate(blank + scaled, axis=1)
        logits_ref[...] = lax.dot_general(
            router_ref[...], xg_ref[...], NT, preferred_element_type=jnp.float32
        )

    rows, wide = w_ref.shape[0], xg_ref.shape[1]
    gate = lax.dot_general(w_ref[:, :wide], xg_ref[...], NT, preferred_element_type=jnp.float32)
    up = lax.dot_general(
        w_ref[:, w_ref.shape[1] - wide :], xu_ref[...], NT, preferred_element_type=jnp.float32
    )
    active = gate * jax.nn.sigmoid(1.702 * gate) * (up + 1.0)
    slabs = act_ref.shape[0]
    for slab in range(slabs):
        act_ref[slab, pl.ds(step * rows, rows), :] = active[:, slab * LANES : (slab + 1) * LANES]

    @pl.when(step == pl.num_programs(1) - 1)
    def _():
        for row in range(halves):
            wanted = pl.ds(row, units, stride=halves) if halves > 1 else pl.ds(0, units)
            picked = jnp.concatenate([act_ref[slab, wanted, :] for slab in range(slabs)], axis=1)
            spread = one_hot_rows(slot_ref[row], out_ref.shape[2], 1.0)
            out_ref[row, 0] = lax.dot_general(
                spread, picked.astype(jnp.bfloat16), NT, preferred_element_type=jnp.float32
            ).astype(jnp.bfloat16)


def gate_up_call(state, gain, router, weights, slots, units, token_block, cap):
    halves = slots.shape[0]
    sources, shards, group_rows, cols = state.shape
    groups = token_block // group_rows
    blocks = sources // groups
    experts, wide = router.shape
    wide_w = weights.shape[1]
    sizes = [
        size
        for size in range(1, units + 1)
        if units % size == 0
        and (size == units or (size * halves) % 16 == 0)
        and size * halves * wide_w * 2 <= 4 << 20
    ]
    size = sizes[-1]
    return pl.pallas_call(
        functools.partial(gate_up_kernel, halves, units),
        grid=(blocks, units // size),
        out_shape=(
            jax.ShapeDtypeStruct((halves, blocks, cap, units), jnp.bfloat16),
            jax.ShapeDtypeStruct((experts, blocks * token_block), jnp.float32),
        ),
        in_specs=[
            pl.BlockSpec((groups, shards, group_rows, cols), lambda i, j: (i, 0, 0, 0)),
            pl.BlockSpec((shards, 1, cols), lambda i, j: (0, 0, 0)),
            pl.BlockSpec((experts, wide), lambda i, j: (0, 0)),
            pl.BlockSpec((size * halves, wide_w), lambda i, j: (j, 0)),
            pl.BlockSpec((halves, 1, token_block), lambda i, j: (0, 0, i)),
        ],
        out_specs=(
            pl.BlockSpec((halves, 1, cap, units), lambda i, j: (0, i, 0, 0)),
            pl.BlockSpec((experts, token_block), lambda i, j: (0, i)),
        ),
        scratch_shapes=[
            pltpu.VMEM((token_block // LANES, units * halves, LANES), jnp.float32),
            pltpu.VMEM((token_block, wide), jnp.bfloat16),
            pltpu.VMEM((token_block, wide), jnp.bfloat16),
        ],
        compiler_params=pltpu.CompilerParams(vmem_limit_bytes=56 << 20),
    )(state, gain, router, weights, slots)


def down_kernel(act_ref, w_ref, slot_ref, mix_ref, out_ref, total_ref):
    step = pl.program_id(1)
    part = None
    for row in range(w_ref.shape[0]):
        pieces = [act_ref[shard, row, 0] for shard in range(act_ref.shape[0])]
        hidden = jnp.concatenate(pieces, axis=1)
        piece = jnp.dot(hidden, w_ref[row], preferred_element_type=jnp.float32)
        part = piece if part is None else part + piece
    spread = one_hot_rows(slot_ref[0], act_ref.shape[3], mix_ref[0])
    added = lax.dot_general(
        spread, part.astype(jnp.bfloat16), TN, preferred_element_type=jnp.float32
    )

    @pl.when(step == 0)
    def _():
        total_ref[...] = added

    @pl.when(step != 0)
    def _():
        total_ref[...] += added

    @pl.when(step == pl.num_programs(1) - 1)
    def _():
        out_ref[...] = total_ref[...].astype(jnp.bfloat16)


def down_call(act, weights, slots, mix, token_block):
    shards, halves, blocks, cap, units = act.shape
    hidden, cols = weights.shape[1:]
    pair = 2 if halves % 2 == 0 else 1
    return pl.pallas_call(
        down_kernel,
        grid=(blocks, halves // pair),
        out_shape=jax.ShapeDtypeStruct((blocks * token_block, cols), jnp.bfloat16),
        in_specs=[
            pl.BlockSpec((shards, pair, 1, cap, units), lambda i, r: (0, r, i, 0, 0)),
            pl.BlockSpec((pair, hidden, cols), lambda i, r: (r, 0, 0)),
            pl.BlockSpec((1, 1, token_block), lambda i, r: (r * pair, 0, i)),
            pl.BlockSpec((1, 1, token_block), lambda i, r: (r * pair, 0, i)),
        ],
        out_specs=pl.BlockSpec((token_block, cols), lambda i, r: (i, 0)),
        scratch_shapes=[pltpu.VMEM((token_block, cols), jnp.float32)],
        compiler_params=pltpu.CompilerParams(vmem_limit_bytes=48 << 20),
    )(act, weights, slots, mix)


def on_device(
    queries, keyvals, sinks, stream, out_weight, norm_gain, router, expert_ids, w_gate_up, w_down
):
    ctx_count = lax.axis_size("ctx")
    rep_count = lax.axis_size("rep")
    share = out_weight.shape[1] // rep_count
    if share * rep_count == out_weight.shape[1]:
        own_share = lax.dynamic_slice_in_dim(
            out_weight, lax.axis_index("rep") * share, share, 1
        )
        full_weight = lax.all_gather(own_share, ("ctx", "rep"), axis=1, tiled=True)
    else:
        full_weight = lax.all_gather(out_weight, "ctx", axis=1, tiled=True)
    local_seqs = queries.shape[0]
    tokens = queries.shape[1]
    row_count = local_seqs * tokens
    kv_local = keyvals.shape[2]
    head_dim = keyvals.shape[3] // 2
    q_local = queries.shape[2] // head_dim
    query_group_size = q_local // kv_local
    wide_rows = query_group_size * tokens
    col_width = stream.shape[2]
    first_pos = lax.axis_index("ctx") * tokens
    last_pos = first_pos + tokens - 1
    score_scale = head_dim ** (-0.5)
    scaled_queries = queries * jnp.asarray(score_scale, jnp.bfloat16)
    query_grid = scaled_queries.reshape(local_seqs, tokens, kv_local, query_group_size, head_dim)
    query_wide = jnp.transpose(query_grid, (0, 2, 3, 1, 4)).reshape(
        local_seqs, kv_local, wide_rows, head_dim
    )
    positions = first_pos + jnp.tile(jnp.arange(tokens), query_group_size)
    sink_rows = jnp.repeat(sinks.reshape(kv_local, query_group_size), tokens, axis=1)
    sink_grid = jnp.broadcast_to(sink_rows[None], (local_seqs, kv_local, wide_rows))
    start_state = (
        sink_grid,
        jnp.ones_like(sink_grid),
        jnp.zeros((local_seqs, kv_local, head_dim, wide_rows), jnp.float32),
    )

    def attend_block(running, shard_piece):
        peak_old, denom_old, accum_old = running
        key_block = shard_piece[..., :head_dim]
        value_block = shard_piece[..., head_dim:]
        scores = jnp.einsum(
            "skmd,snkd->sknm", query_wide, key_block, preferred_element_type=jnp.float32
        )
        key_pos = jnp.arange(shard_piece.shape[1])
        visible = key_pos[:, None] <= positions[None, :]
        masked = jnp.where(visible[None, None], scores, -jnp.inf)
        peak_new = jnp.maximum(peak_old, jnp.max(masked, axis=2))
        exp_terms = jnp.exp(masked - peak_new[:, :, None, :])
        factor = jnp.exp(peak_old - peak_new)
        denom_new = denom_old * factor + jnp.sum(exp_terms, axis=2)
        accum_new = accum_old * factor[:, :, None, :] + jnp.einsum(
            "sknm,snkd->skdm",
            exp_terms.astype(jnp.bfloat16),
            value_block,
            preferred_element_type=jnp.float32,
        )
        return (peak_new, denom_new, accum_new)

    shard_piece = lax.all_gather(keyvals, "ctx", axis=1, tiled=True)

    def keep_state(state_in):
        return state_in

    def update_state(state_in):
        return attend_block(state_in, shard_piece)

    peak_fin, denom_fin, accum_fin = lax.cond(
        jnp.int32(0) > last_pos, keep_state, update_state, start_state
    )
    normalized = (accum_fin / denom_fin[:, :, None, :]).reshape(
        local_seqs, kv_local, head_dim, query_group_size, tokens
    )
    attended = (
        jnp.transpose(normalized, (0, 4, 1, 3, 2))
        .reshape(row_count, q_local * head_dim)
        .astype(jnp.bfloat16)
    )
    token_ids = lax.all_gather(
        expert_ids.reshape(row_count, expert_ids.shape[2]).T, "ctx", axis=1, tiled=True
    )
    all_rows = ctx_count * row_count
    halves = w_gate_up.shape[0]
    units = w_gate_up.shape[1]
    token_block = min(all_rows, 8 * tokens)
    cap = token_block // tokens * (3 * tokens // 16)
    row_expert = (lax.axis_index("ctx") * halves + jnp.arange(halves)) // 2
    named = jnp.any(token_ids[:, None, :] == row_expert[None, :, None], axis=0)
    counted = named.astype(jnp.int32).reshape(halves, all_rows // token_block, token_block)
    rank = jnp.cumsum(counted, axis=2) - 1
    slots = jnp.where(named, rank.reshape(halves, all_rows), -1).reshape(halves, 1, all_rows)
    attended, slots, token_ids = lax.optimization_barrier((attended, slots, token_ids))
    partial_proj = jnp.dot(attended, full_weight, preferred_element_type=jnp.float32)
    own_stream = stream.reshape(row_count, col_width).astype(jnp.float32)
    summed = lax.psum_scatter(
        partial_proj.astype(jnp.bfloat16), "head", scatter_dimension=1, tiled=True
    )
    own_state = (summed.astype(jnp.float32) + own_stream).astype(jnp.bfloat16)
    width = norm_gain.shape[0]
    every_state = lax.all_gather(own_state, ("ctx", "head"), axis=0, tiled=False)
    every_state = every_state.reshape(ctx_count, width // col_width, row_count, col_width)
    expert_count = router.shape[1]
    unit_rows = jnp.transpose(w_gate_up, (1, 0, 2)).reshape(units * halves, w_gate_up.shape[2])
    router_rows = jnp.pad(router.T, ((0, 0), (0, -width % LANES)))
    gain = norm_gain.reshape(width // col_width, 1, col_width)
    active, logits = gate_up_call(
        every_state, gain, router_rows, unit_rows, slots, units, token_block, cap
    )
    member = jnp.any(token_ids[:, None, :] == jnp.arange(expert_count)[None, :, None], axis=0)
    masked = jnp.where(member, logits, -jnp.inf)
    mix_all = jax.nn.softmax(masked, axis=0)
    chosen_rows = (row_expert[:, None] == jnp.arange(expert_count)[None, :]).astype(jnp.float32)
    mix_rows = jnp.dot(chosen_rows, mix_all, precision=lax.Precision.HIGHEST)
    mix_rows = mix_rows.reshape(halves, 1, all_rows)
    every_active = lax.all_gather(active.reshape(-1, units), "head", axis=0, tiled=True)
    every_active = every_active.reshape(width // col_width, *active.shape)
    partial_out = down_call(every_active, w_down, slots, mix_rows, token_block)
    combined = lax.psum_scatter(partial_out, "ctx", scatter_dimension=0, tiled=True)
    layer_out = (own_state.astype(jnp.float32) + combined.astype(jnp.float32)).astype(jnp.bfloat16)
    return layer_out.reshape(local_seqs, tokens, col_width)


def solution(mesh):
    placed = (
        P("rep", "ctx", "head"),
        P("rep", "ctx", "head", None),
        P("head"),
        P("rep", "ctx", "head"),
        P("head", "ctx"),
        P(),
        P(),
        P("rep", "ctx", None),
        P("ctx", "head", None),
        P("ctx", None, "head"),
    )
    return jax.shard_map(
        on_device, mesh=mesh, in_specs=placed, out_specs=P("rep", "ctx", "head"), check_vma=False
    )
```

```python
import functools

import jax
import jax.numpy as jnp
from jax import lax
from jax.experimental import pallas as pl
from jax.experimental.pallas import tpu as pltpu
from jax.sharding import PartitionSpec as P


NT = (((1,), (1,)), ((), ()))
TN = (((0,), (0,)), ((), ()))
LANES = 128


def one_hot_rows(slots, cap, value):
    rows = lax.broadcasted_iota(jnp.int32, (cap, slots.shape[1]), 0)
    return jnp.where(rows == slots, value, 0.0).astype(jnp.bfloat16)


def gate_up_kernel(
    halves,
    units,
    state_ref,
    gain_ref,
    router_ref,
    w_ref,
    slot_ref,
    out_ref,
    logits_ref,
    act_ref,
    xg_ref,
    xu_ref,
):
    step = pl.program_id(1)
    groups, shards, group_rows, cols = state_ref.shape

    @pl.when(step == 0)
    def _():
        for group in range(groups):
            pieces = [state_ref[group, shard].astype(jnp.float32) for shard in range(shards)]
            square = sum(jnp.sum(piece * piece, axis=1, keepdims=True) for piece in pieces)
            inverse = lax.rsqrt(square / (shards * cols) + 1e-05)
            scaled = [
                (piece * inverse * gain_ref[shard]).astype(jnp.bfloat16)
                for shard, piece in enumerate(pieces)
            ]
            extra = xg_ref.shape[1] - shards * cols
            blank = [jnp.zeros((group_rows, extra), jnp.bfloat16)] if extra else []
            here = slice(group * group_rows, (group + 1) * group_rows)
            xg_ref[here, :] = jnp.concatenate(scaled + blank, axis=1)
            xu_ref[here, :] = jnp.concatenate(blank + scaled, axis=1)
        logits_ref[...] = lax.dot_general(
            router_ref[...], xg_ref[...], NT, preferred_element_type=jnp.float32
        )

    rows, wide = w_ref.shape[0], xg_ref.shape[1]
    gate = lax.dot_general(w_ref[:, :wide], xg_ref[...], NT, preferred_element_type=jnp.float32)
    up = lax.dot_general(
        w_ref[:, w_ref.shape[1] - wide :], xu_ref[...], NT, preferred_element_type=jnp.float32
    )
    active = gate * jax.nn.sigmoid(1.702 * gate) * (up + 1.0)
    slabs = act_ref.shape[0]
    for slab in range(slabs):
        act_ref[slab, pl.ds(step * rows, rows), :] = active[:, slab * LANES : (slab + 1) * LANES]

    @pl.when(step == pl.num_programs(1) - 1)
    def _():
        for row in range(halves):
            wanted = pl.ds(row, units, stride=halves) if halves > 1 else pl.ds(0, units)
            picked = jnp.concatenate([act_ref[slab, wanted, :] for slab in range(slabs)], axis=1)
            spread = one_hot_rows(slot_ref[row], out_ref.shape[2], 1.0)
            out_ref[row, 0] = lax.dot_general(
                spread, picked.astype(jnp.bfloat16), NT, preferred_element_type=jnp.float32
            ).astype(jnp.bfloat16)


def gate_up_call(state, gain, router, weights, slots, units, token_block, cap):
    halves = slots.shape[0]
    sources, shards, group_rows, cols = state.shape
    groups = token_block // group_rows
    blocks = sources // groups
    experts, wide = router.shape
    wide_w = weights.shape[1]
    sizes = [
        size
        for size in range(1, units + 1)
        if units % size == 0
        and (size == units or (size * halves) % 16 == 0)
        and size * halves * wide_w * 2 <= 4 << 20
    ]
    size = sizes[-1]
    return pl.pallas_call(
        functools.partial(gate_up_kernel, halves, units),
        grid=(blocks, units // size),
        out_shape=(
            jax.ShapeDtypeStruct((halves, blocks, cap, units), jnp.bfloat16),
            jax.ShapeDtypeStruct((experts, blocks * token_block), jnp.float32),
        ),
        in_specs=[
            pl.BlockSpec((groups, shards, group_rows, cols), lambda i, j: (i, 0, 0, 0)),
            pl.BlockSpec((shards, 1, cols), lambda i, j: (0, 0, 0)),
            pl.BlockSpec((experts, wide), lambda i, j: (0, 0)),
            pl.BlockSpec((size * halves, wide_w), lambda i, j: (j, 0)),
            pl.BlockSpec((halves, 1, token_block), lambda i, j: (0, 0, i)),
        ],
        out_specs=(
            pl.BlockSpec((halves, 1, cap, units), lambda i, j: (0, i, 0, 0)),
            pl.BlockSpec((experts, token_block), lambda i, j: (0, i)),
        ),
        scratch_shapes=[
            pltpu.VMEM((token_block // LANES, units * halves, LANES), jnp.float32),
            pltpu.VMEM((token_block, wide), jnp.bfloat16),
            pltpu.VMEM((token_block, wide), jnp.bfloat16),
        ],
        compiler_params=pltpu.CompilerParams(vmem_limit_bytes=56 << 20),
    )(state, gain, router, weights, slots)


def down_kernel(act_ref, w_ref, slot_ref, mix_ref, out_ref, total_ref):
    step = pl.program_id(1)
    part = None
    for row in range(w_ref.shape[0]):
        pieces = [act_ref[shard, row, 0] for shard in range(act_ref.shape[0])]
        hidden = jnp.concatenate(pieces, axis=1)
        piece = jnp.dot(hidden, w_ref[row], preferred_element_type=jnp.float32)
        part = piece if part is None else part + piece
    spread = one_hot_rows(slot_ref[0], act_ref.shape[3], mix_ref[0])
    added = lax.dot_general(
        spread, part.astype(jnp.bfloat16), TN, preferred_element_type=jnp.float32
    )

    @pl.when(step == 0)
    def _():
        total_ref[...] = added

    @pl.when(step != 0)
    def _():
        total_ref[...] += added

    @pl.when(step == pl.num_programs(1) - 1)
    def _():
        out_ref[...] = total_ref[...].astype(jnp.bfloat16)


def down_call(act, weights, slots, mix, token_block):
    shards, halves, blocks, cap, units = act.shape
    hidden, cols = weights.shape[1:]
    pair = 2 if halves % 2 == 0 else 1
    return pl.pallas_call(
        down_kernel,
        grid=(blocks, halves // pair),
        out_shape=jax.ShapeDtypeStruct((blocks * token_block, cols), jnp.bfloat16),
        in_specs=[
            pl.BlockSpec((shards, pair, 1, cap, units), lambda i, r: (0, r, i, 0, 0)),
            pl.BlockSpec((pair, hidden, cols), lambda i, r: (r, 0, 0)),
            pl.BlockSpec((1, 1, token_block), lambda i, r: (r * pair, 0, i)),
            pl.BlockSpec((1, 1, token_block), lambda i, r: (r * pair, 0, i)),
        ],
        out_specs=pl.BlockSpec((token_block, cols), lambda i, r: (i, 0)),
        scratch_shapes=[pltpu.VMEM((token_block, cols), jnp.float32)],
        compiler_params=pltpu.CompilerParams(vmem_limit_bytes=48 << 20),
    )(act, weights, slots, mix)


def on_device(
    queries, keyvals, sinks, stream, out_weight, norm_gain, router, expert_ids, w_gate_up, w_down
):
    ctx_count = lax.axis_size("ctx")
    local_seqs = queries.shape[0]
    tokens = queries.shape[1]
    row_count = local_seqs * tokens
    kv_local = keyvals.shape[2]
    head_dim = keyvals.shape[3] // 2
    q_local = queries.shape[2] // head_dim
    query_group_size = q_local // kv_local
    wide_rows = query_group_size * tokens
    col_width = stream.shape[2]
    first_pos = lax.axis_index("ctx") * tokens
    last_pos = first_pos + tokens - 1
    score_scale = head_dim ** (-0.5)
    scaled_queries = queries * jnp.asarray(score_scale, jnp.bfloat16)
    query_grid = scaled_queries.reshape(local_seqs, tokens, kv_local, query_group_size, head_dim)
    query_wide = jnp.transpose(query_grid, (0, 2, 3, 1, 4)).reshape(
        local_seqs, kv_local, wide_rows, head_dim
    )
    positions = first_pos + jnp.tile(jnp.arange(tokens), query_group_size)
    sink_rows = jnp.repeat(sinks.reshape(kv_local, query_group_size), tokens, axis=1)
    sink_grid = jnp.broadcast_to(sink_rows[None], (local_seqs, kv_local, wide_rows))
    start_state = (
        sink_grid,
        jnp.ones_like(sink_grid),
        jnp.zeros((local_seqs, kv_local, head_dim, wide_rows), jnp.float32),
    )

    def attend_block(running, shard_piece):
        peak_old, denom_old, accum_old = running
        key_block = shard_piece[..., :head_dim]
        value_block = shard_piece[..., head_dim:]
        scores = jnp.einsum(
            "skmd,snkd->sknm", query_wide, key_block, preferred_element_type=jnp.float32
        )
        key_pos = jnp.arange(shard_piece.shape[1])
        visible = key_pos[:, None] <= positions[None, :]
        masked = jnp.where(visible[None, None], scores, -jnp.inf)
        peak_new = jnp.maximum(peak_old, jnp.max(masked, axis=2))
        exp_terms = jnp.exp(masked - peak_new[:, :, None, :])
        factor = jnp.exp(peak_old - peak_new)
        denom_new = denom_old * factor + jnp.sum(exp_terms, axis=2)
        accum_new = accum_old * factor[:, :, None, :] + jnp.einsum(
            "sknm,snkd->skdm",
            exp_terms.astype(jnp.bfloat16),
            value_block,
            preferred_element_type=jnp.float32,
        )
        return (peak_new, denom_new, accum_new)

    shard_piece = lax.all_gather(keyvals, "ctx", axis=1, tiled=True)

    def keep_state(state_in):
        return state_in

    def update_state(state_in):
        return attend_block(state_in, shard_piece)

    peak_fin, denom_fin, accum_fin = lax.cond(
        jnp.int32(0) > last_pos, keep_state, update_state, start_state
    )
    normalized = (accum_fin / denom_fin[:, :, None, :]).reshape(
        local_seqs, kv_local, head_dim, query_group_size, tokens
    )
    attended = (
        jnp.transpose(normalized, (0, 4, 1, 3, 2))
        .reshape(row_count, q_local * head_dim)
        .astype(jnp.bfloat16)
    )
    token_ids = lax.all_gather(
        expert_ids.reshape(row_count, expert_ids.shape[2]).T, "ctx", axis=1, tiled=True
    )
    all_rows = ctx_count * row_count
    halves = w_gate_up.shape[0]
    units = w_gate_up.shape[1]
    token_block = min(all_rows, 8 * tokens)
    cap = token_block // tokens * (3 * tokens // 16)
    row_expert = (lax.axis_index("ctx") * halves + jnp.arange(halves)) // 2
    named = jnp.any(token_ids[:, None, :] == row_expert[None, :, None], axis=0)
    counted = named.astype(jnp.int32).reshape(halves, all_rows // token_block, token_block)
    rank = jnp.cumsum(counted, axis=2) - 1
    slots = jnp.where(named, rank.reshape(halves, all_rows), -1).reshape(halves, 1, all_rows)
    width = norm_gain.shape[0]
    head_count = lax.axis_size("head")
    swapped = ctx_count == head_count and out_weight.shape[1] == col_width
    if swapped:
        pairs = [
            (first * head_count + second, second * head_count + first)
            for first in range(ctx_count)
            for second in range(head_count)
        ]
        turned = lax.ppermute(
            stream.reshape(row_count, col_width), ("ctx", "head"), perm=pairs
        )
        every_row = lax.all_gather(attended, "ctx", axis=0, tiled=True)
        partial_proj = jnp.dot(every_row, out_weight, preferred_element_type=jnp.float32)
        summed = lax.psum_scatter(
            partial_proj.astype(jnp.bfloat16), "head", scatter_dimension=0, tiled=True
        )
        turned_state = summed.astype(jnp.float32) + turned.astype(jnp.float32)
        every_state = lax.all_gather(
            turned_state.astype(jnp.bfloat16), ("head", "ctx"), axis=0, tiled=False
        )
    else:
        partial_proj = jnp.dot(attended, lax.all_gather(out_weight, "ctx", axis=1, tiled=True), preferred_element_type=jnp.float32)
        own_stream = stream.reshape(row_count, col_width).astype(jnp.float32)
        summed = lax.psum_scatter(
            partial_proj.astype(jnp.bfloat16), "head", scatter_dimension=1, tiled=True
        )
        own_state = (summed.astype(jnp.float32) + own_stream).astype(jnp.bfloat16)
        every_state = lax.all_gather(own_state, ("ctx", "head"), axis=0, tiled=False)
    every_state = every_state.reshape(ctx_count, width // col_width, row_count, col_width)
    expert_count = router.shape[1]
    unit_rows = jnp.transpose(w_gate_up, (1, 0, 2)).reshape(units * halves, w_gate_up.shape[2])
    router_rows = jnp.pad(router.T, ((0, 0), (0, -width % LANES)))
    gain = norm_gain.reshape(width // col_width, 1, col_width)
    active, logits = gate_up_call(
        every_state, gain, router_rows, unit_rows, slots, units, token_block, cap
    )
    member = jnp.any(token_ids[:, None, :] == jnp.arange(expert_count)[None, :, None], axis=0)
    masked = jnp.where(member, logits, -jnp.inf)
    mix_all = jax.nn.softmax(masked, axis=0)
    chosen_rows = (row_expert[:, None] == jnp.arange(expert_count)[None, :]).astype(jnp.float32)
    mix_rows = jnp.dot(chosen_rows, mix_all, precision=lax.Precision.HIGHEST)
    mix_rows = mix_rows.reshape(halves, 1, all_rows)
    every_active = lax.all_gather(active.reshape(-1, units), "head", axis=0, tiled=True)
    every_active = every_active.reshape(width // col_width, *active.shape)
    partial_out = down_call(every_active, w_down, slots, mix_rows, token_block)
    combined = lax.psum_scatter(partial_out, "ctx", scatter_dimension=0, tiled=True)
    if swapped:
        own_state = every_state[lax.axis_index("ctx"), lax.axis_index("head")]
    layer_out = (own_state.astype(jnp.float32) + combined.astype(jnp.float32)).astype(jnp.bfloat16)
    return layer_out.reshape(local_seqs, tokens, col_width)


def solution(mesh):
    placed = (
        P("rep", "ctx", "head"),
        P("rep", "ctx", "head", None),
        P("head"),
        P("rep", "ctx", "head"),
        P("head", "ctx"),
        P(),
        P(),
        P("rep", "ctx", None),
        P("ctx", "head", None),
        P("ctx", None, "head"),
    )
    return jax.shard_map(
        on_device, mesh=mesh, in_specs=placed, out_specs=P("rep", "ctx", "head"), check_vma=False
    )
```
